512 devices in a mesh: vol: 8 (over x, core), row: 16 (over y, z_hi), col: 4 (over z_lo).
Axes of the slice: x: 4, y: 4, z: 16 (z_hi: 4, z_lo: 4; z = z_hi * 4 + z_lo), core: 2. Of those that a mesh axis runs over, the one named last changes fastest.
Arguments:
- source: float32 [16, 64, 128, 512], P(None, 'vol', 'row', 'col'), may hold values from -8 to 8
- labels: int32 [64, 128, 512], P('vol', 'row', 'col'), may hold values from 0 to 7
- region_coeff: float32 [8], replicated, may hold values from 0.3 to 3
- node_cell: int32 [65536], P(('vol', 'row', 'col')), may hold values from 0 to 8191
- node_pos: float32 [3, 65536], P(None, ('vol', 'row', 'col')), may hold values from 0 to 1
- incident: float32 [16, 65536], P(None, ('vol', 'row', 'col')), may hold values from -6 to 6
Outputs:
- field: float32 [16, 64, 128, 512], P(None, 'vol', 'row', 'col')
- flux: float32 [16, 65536], P(None, ('vol', 'row', 'col'))
The draws below stay inside these ranges and needn't reach their ends.
Inputs may be any that keep to these rules, and one draw needn't show every extreme that they name: `node_cell`: cell of node j inside its volume block, several nodes may share a cell.
All inputs are finite; a program needn't handle non-finite values.
Results may differ from the reference program's by a relative error of at most 0.0029.
Values may be sent and summed in bfloat16 or wider, within the bound.
A program may use at most 64 MiB of HBM per device.

```python
import math
import jax
import jax.numpy as jnp
from jax import lax

E = 16
REGIONS = 8
NODE_DEV = 128
CX = 8
CY = 8
CZ = 128
SWEEPS = 4
ITERS = 2
NX = 64
NY = 128
NZ = 512
M = 65536
N_ROW = 16
N_COL = 4


def with_ends(array, rng, least, largest):
    place = [jax.random.randint(jax.random.fold_in(rng, axis), (), 0, length) for axis, length in enumerate(array.shape)]
    longest = array.shape.index(max(array.shape))
    neighbour = place[:longest] + [(place[longest] + 1) % array.shape[longest]] + place[longest + 1:]
    return array.at[tuple(place)].set(least).at[tuple(neighbour)].set(largest)


def levels(stream_key, dims, cuts, least, top_value):
    level, own = 1.0, jax.random.fold_in(stream_key, 6)
    for dim, blocks in cuts:
        heights = jnp.exp(jax.random.uniform(jax.random.fold_in(own, dim), (blocks,), jnp.float32, least / len(cuts), top_value / len(cuts)))
        level = level * jnp.repeat(heights, dims[dim] // blocks).reshape([-1 if axis == dim else 1 for axis in range(len(dims))])
    return level


def gaussian(stream_key, extent, spread, limit, shards=(), held_as=jnp.bfloat16):
    drawn = jax.random.normal(stream_key, extent, jnp.float32) * spread
    if len(shards) > 0:
        drawn = levels(stream_key, extent, shards, -0.22, 0.18) * drawn
    return jnp.clip(drawn, min=-limit, max=limit).astype(held_as)


def setup_inputs(seed: int = 0) -> dict:
    arg_keys = jax.random.split(jax.random.key(seed), 7)
    return {
        "source": gaussian(arg_keys[0], (E, NX, NY, NZ), 1.0, 8.0, ((1, 8), (2, 16), (3, 4)), jnp.float32),
        "labels": with_ends(jax.random.randint(arg_keys[1], (NX, NY, NZ), 0, REGIONS), jax.random.fold_in(arg_keys[1], 1), 0, REGIONS - 1).astype(jnp.int32),
        "region_coeff": jnp.clip(jnp.exp(jax.random.uniform(arg_keys[2], (REGIONS,), jnp.float32, math.log(0.3), math.log(3.0))), 0.3, 3.0),
        "node_cell": with_ends(jax.random.randint(arg_keys[3], (M,), 0, CX * CY * CZ), jax.random.fold_in(arg_keys[3], 1), 0, (CX * CY * CZ) - 1).astype(jnp.int32),
        "node_pos": jnp.clip(1.0 * jax.random.uniform(arg_keys[4], (3, M), jnp.float32) ** levels(arg_keys[4], (3, M), ((1, 512),), -0.2, 0.2), 0.0, 1.0),
        "incident": gaussian(arg_keys[5], (E, M), 1.0, 6.0, ((1, 512),), jnp.float32),
    }


MASS_TERM = 0.05
SOFTENING = 0.05
KERNEL_GAIN = 2.0
COUPLING = 1.0

def sweep_weights(count):
    return [1.0 / (1.05 - 0.95 * math.cos(math.pi * (2 * sweep + 1) / (2 * count))) for sweep in range(count)]

def face_terms(kcoef):
    padded = jnp.pad(kcoef, 1)
    neighbours = [padded[2:, 1:-1, 1:-1], padded[:-2, 1:-1, 1:-1], padded[1:-1, 2:, 1:-1], padded[1:-1, :-2, 1:-1], padded[1:-1, 1:-1, 2:], padded[1:-1, 1:-1, :-2]]
    faces = [0.5 * (kcoef + other) for other in neighbours]
    diag = MASS_TERM + faces[0]
    for other in faces[1:]:
        diag = diag + other
    return (faces, diag)

def operate(values, faces, diag):
    padded = jnp.pad(values, ((0, 0), (1, 1), (1, 1), (1, 1)))
    neighbours = [padded[:, 2:, 1:-1, 1:-1], padded[:, :-2, 1:-1, 1:-1], padded[:, 1:-1, 2:, 1:-1], padded[:, 1:-1, :-2, 1:-1], padded[:, 1:-1, 1:-1, 2:], padded[:, 1:-1, 1:-1, :-2]]
    total = faces[0] * neighbours[0]
    for number in range(1, 6):
        total = total + faces[number] * neighbours[number]
    return diag * values - total

def node_index(node_cell):
    nodes = jnp.arange(M, dtype=jnp.int32)
    block = nodes // NODE_DEV
    block_x = block // (N_ROW * N_COL)
    block_y = block // N_COL % N_ROW
    block_z = block % N_COL
    local_x = node_cell // (CY * CZ)
    local_y = node_cell // CZ % CY
    local_z = node_cell % CZ
    global_x = block_x * CX + local_x
    global_y = block_y * CY + local_y
    global_z = block_z * CZ + local_z
    return ((global_x * NY + global_y) * NZ + global_z).astype(jnp.int32)

def surface_product(traces, node_pos):
    scale = KERNEL_GAIN / math.sqrt(M)
    blocking = math.gcd(M, 1024)
    blocks = node_pos.reshape(3, M // blocking, blocking).transpose(1, 0, 2)
    wide_traces = lax.optimization_barrier(traces).astype(jnp.float32)

    def one_block(block_pos):
        delta_x = node_pos[0][:, None] - block_pos[0][None, :]
        delta_y = node_pos[1][:, None] - block_pos[1][None, :]
        delta_z = node_pos[2][:, None] - block_pos[2][None, :]
        squared = delta_x * delta_x + delta_y * delta_y + delta_z * delta_z
        tile = (scale * lax.rsqrt(squared + SOFTENING * SOFTENING)).astype(jnp.bfloat16)
        wide_tile = lax.optimization_barrier(tile).astype(jnp.float32)
        return jnp.dot(wide_traces, wide_tile, preferred_element_type=jnp.float32)
    result = lax.map(one_block, blocks)
    return result.transpose(1, 0, 2).reshape(traces.shape[0], M)

def reference(source, labels, region_coeff, node_cell, node_pos, incident):
    kcoef = region_coeff[labels]
    faces, diag = face_terms(kcoef)
    flat = node_index(node_cell)
    field = jnp.zeros(source.shape, jnp.float32)
    flux = incident
    weights = sweep_weights(SWEEPS)
    for outer in range(ITERS):
        rhs = source.reshape(E, -1).at[:, flat].add(COUPLING * flux).reshape(source.shape)
        for weight in weights:
            field = field + weight * (rhs - operate(field, faces, diag)) / diag
        traces = field.reshape(E, -1)[:, flat].astype(jnp.bfloat16)
        flux = incident + surface_product(traces, node_pos)
    return (field, flux)
```

```python
import functools
import math

import jax
import jax.numpy as jnp
from jax import lax
from jax.experimental import pallas as pl
from jax.experimental.pallas import tpu as pltpu
from jax.sharding import PartitionSpec as P

SWEEPS = 4
ITERS = 2

MASS_TERM = 0.05
SOFTENING = 0.05
KERNEL_GAIN = 2.0

MESH = pl.DeviceIdType.MESH
F32 = jnp.float32
BF16 = jnp.bfloat16

E, CX, CY, CZ, ND = 16, 8, 8, 128, 128
STEPS = SWEEPS * ITERS
HALOS = STEPS - 1


def sweep_weights(count):
    return [
        1.0 / (1.05 - 0.95 * math.cos(math.pi * (2 * sweep + 1) / (2 * count)))
        for sweep in range(count)
    ]


class Plan:
    def __init__(self, mesh):
        self.n_vol, self.n_row, self.n_col = (mesh.shape[a] for a in ("vol", "row", "col"))
        self.z_hi = 4 if self.n_row == 16 else 2
        self.n_y = self.n_row // self.z_hi
        self.n_z = self.z_hi * self.n_col
        half = self.n_z // 2
        order = []
        for d in range(1, half):
            order += [d, self.n_z - d]
        order += [0, half]
        self.z_deltas = order
        self.z_own = order.index(0)
        self.n_q = self.n_z // 2
        ring = lambda d, n: min(d, n - d)
        plane = [(dv, dy) for dv in range(self.n_vol) for dy in range(self.n_y)]
        plane.sort(key=lambda p: -(ring(p[0], self.n_vol) / 2 + ring(p[1], self.n_y)))
        self.p_deltas = plane
        self.p_own = plane.index((0, 0))
        self.n_p = len(plane)
        self.n_m = self.n_p // 2
        self.nodes = ND * self.n_vol * self.n_row * self.n_col

    def here(self):
        v, r, c = (lax.axis_index(a) for a in ("vol", "row", "col"))
        self.v, self.r, self.c = v, r, c
        self.y = lax.div(r, self.z_hi)
        self.zh = lax.rem(r, self.z_hi)
        self.z = self.zh * self.n_col + c

    def z_peer(self, delta):
        zz = lax.rem(self.z + delta, self.n_z)
        return (self.v, self.y * self.z_hi + lax.div(zz, self.n_col), lax.rem(zz, self.n_col))

    def p_peer(self, delta):
        dv, dy = delta
        return (
            lax.rem(self.v + dv, self.n_vol),
            lax.rem(self.y + dy, self.n_y) * self.z_hi + self.zh,
            self.c,
        )

    def z_slot_of_me_at(self, delta):
        return self.z_deltas.index((self.n_z - delta) % self.n_z)

    def p_slot_of_me_at(self, delta):
        return self.p_deltas.index(((self.n_vol - delta[0]) % self.n_vol, (self.n_y - delta[1]) % self.n_y))

    def sides(self):
        up = lambda i, n: lax.rem(i + 1, n)
        down = lambda i, n: lax.rem(i + n - 1, n)
        v, r, c = self.v, self.r, self.c
        return (
            (up(v, self.n_vol), r, c),
            (down(v, self.n_vol), r, c),
            (v, up(r, self.n_row), c),
            (v, down(r, self.n_row), c),
            (v, r, up(c, self.n_col)),
            (v, r, down(c, self.n_col)),
        )


def kernel(
    plan, source, labels, coeff, cell, pos, incident, field_out, flux_out,
    F, S, B, KC, KYS, KYR, KZS, KZR, CO, DI, YS, YR, ZS, ZR, OH, TR, ACC, RR, G, POSZ, POSP, PJ,
    src_sem, out_sem, k_ss, k_rs, h_ss, h_rs, pz_ss, pz_rs, pp_ss, pp_rs, t_ss, t_rs, r_ss, r_rs,
):
    plan.here()
    weights = sweep_weights(SWEEPS) * ITERS
    lanes = lax.broadcasted_iota(jnp.int32, (8, 128), 1)
    subs = lax.broadcasted_iota(jnp.int32, (8, 128), 0)
    sides = plan.sides()
    n_q, n_m, n_p, n_z = plan.n_q, plan.n_m, plan.n_p, plan.n_z

    def source_copy(x, y):
        return pltpu.make_async_copy(source.at[:, x, y, :], S.at[x, y], src_sem)

    def field_copy(x, y):
        return pltpu.make_async_copy(F.at[STEPS - 1, x + 1, y + 1], field_out.at[:, x, y, :], out_sem)

    def over_blocks(act):
        def body(x, _):
            for y in range(CY):
                act(x, y)
            return 0

        lax.fori_loop(0, CX, body, 0)

    over_blocks(lambda x, y: source_copy(x, y).start())

    barrier = pltpu.get_barrier_semaphore()
    peers = [plan.z_peer(d) for d in plan.z_deltas if d]
    peers += [plan.p_peer(d) for d in plan.p_deltas if d != (0, 0)]
    peers += [sides[2], sides[3]]
    for peer in peers:
        pl.semaphore_signal(barrier, inc=1, device_id=peer, device_id_type=MESH)

    kz_up = jnp.zeros((8, 128), F32)
    kz_down = jnp.zeros((8, 128), F32)
    for x in range(CX):
        label = labels[x]
        k = jnp.zeros((8, 128), F32)
        for region in range(8):
            k = jnp.where(label == region, coeff[region], k)
        KC[x + 1] = k
        KYS[0, x] = k[CY - 1]
        KYS[1, x] = k[0]
        kz_up = jnp.where(lanes == x, pltpu.roll(k, x + 1, 1), kz_up)
        kz_down = jnp.where(lanes == x, pltpu.roll(k, x, 1), kz_down)
    KZS[0] = kz_up
    KZS[1] = kz_down

    inverse_scale = math.sqrt(plan.nodes) / KERNEL_GAIN
    own_pos = jnp.concatenate([pos[...] * inverse_scale, jnp.zeros((5, 128), F32)], axis=0)
    POSZ[plan.z_own] = own_pos
    POSP[plan.p_own] = own_pos
    cells = jnp.broadcast_to(cell[...], (8, 128))
    rows = lax.div(cells, CZ)
    rows16 = jnp.concatenate([rows, rows], axis=0)
    z_of = lax.rem(cells, CZ)
    for block in range(CZ // 16):
        z_pair = jnp.concatenate([z_of - subs - 16 * block, z_of - subs - 16 * block - 8], axis=0)
        OH[16 * block : 16 * block + 16, :] = jnp.where(z_pair == 0, 1.0, 0.0).astype(BF16)

    pl.semaphore_wait(barrier, len(peers))

    def k_copy(side):
        src, dst = (
            (KC.at[CX], KC.at[0]),
            (KC.at[1], KC.at[CX + 1]),
            (KYS.at[0], KYR.at[0]),
            (KYS.at[1], KYR.at[1]),
            (KZS.at[0], KZR.at[0]),
            (KZS.at[1], KZR.at[1]),
        )[side]
        return pltpu.make_async_remote_copy(
            src_ref=src, dst_ref=dst, send_sem=k_ss.at[side], recv_sem=k_rs.at[side],
            device_id=sides[side], device_id_type=MESH,
        )

    def h_copy(step, side):
        inner = pl.ds(1, CY)
        src, dst = (
            (F.at[step, CX, inner], F.at[step, 0, inner]),
            (F.at[step, 1, inner], F.at[step, CX + 1, inner]),
            (YS.at[step, 0], YR.at[step, 0]),
            (YS.at[step, 1], YR.at[step, 1]),
            (ZS.at[step, 0], ZR.at[step, 0]),
            (ZS.at[step, 1], ZR.at[step, 1]),
        )[side]
        return pltpu.make_async_remote_copy(
            src_ref=src, dst_ref=dst, send_sem=h_ss.at[step, side], recv_sem=h_rs.at[step, side],
            device_id=sides[side], device_id_type=MESH,
        )

    def pz_copy(delta):
        slot = plan.z_slot_of_me_at(delta)
        return pltpu.make_async_remote_copy(
            src_ref=POSZ.at[plan.z_own], dst_ref=POSZ.at[slot], send_sem=pz_ss.at[slot], recv_sem=pz_rs.at[slot],
            device_id=plan.z_peer(delta), device_id_type=MESH,
        )

    def pp_copy(delta):
        slot = plan.p_slot_of_me_at(delta)
        return pltpu.make_async_remote_copy(
            src_ref=POSP.at[plan.p_own], dst_ref=POSP.at[slot], send_sem=pp_ss.at[slot], recv_sem=pp_rs.at[slot],
            device_id=plan.p_peer(delta), device_id_type=MESH,
        )

    def t_slot(it, slot):
        return TR.at[it, slot // 2, :, pl.ds((slot % 2) * ND, ND)]

    def t_copy(it, delta):
        slot = plan.z_slot_of_me_at(delta)
        return pltpu.make_async_remote_copy(
            src_ref=t_slot(it, plan.z_own), dst_ref=t_slot(it, slot), send_sem=t_ss.at[it, slot],
            recv_sem=t_rs.at[it, slot], device_id=plan.z_peer(delta), device_id_type=MESH,
        )

    def r_copy(it, slot):
        return pltpu.make_async_remote_copy(
            src_ref=ACC.at[it, slot], dst_ref=RR.at[it, slot], send_sem=r_ss.at[it, slot],
            recv_sem=r_rs.at[it, slot], device_id=plan.p_peer(plan.p_deltas[slot]), device_id_type=MESH,
        )

    y_first = (2, 3, 0, 1, 4, 5)
    far_first = sorted((d for d in plan.z_deltas if d), key=lambda d: -min(d, n_z - d))
    for side in y_first:
        k_copy(side).start()
    for delta in far_first:
        pz_copy(delta).start()
    for delta in plan.p_deltas:
        if delta != (0, 0):
            pp_copy(delta).start()

    def add_nodes(flux, scaled):
        hi = flux.astype(BF16).astype(F32)
        mid = (flux - hi).astype(BF16).astype(F32)
        low = (flux - hi) - mid

        def body(x, _):
            total = jnp.zeros((CY * E, CZ), F32)
            for part in (hi, mid, low):
                picked = [jnp.where(rows16 == x * CY + y, part, 0.0) for y in range(CY)]
                left = jnp.concatenate(picked, axis=0).astype(BF16)
                total = total + lax.dot_general(
                    left, OH[...], (((1,), (1,)), ((), ())), preferred_element_type=F32
                )
            for y in range(CY):
                b = S[x, y] + total[y * E : (y + 1) * E]
                if scaled:
                    b = b * DI[pl.ds(x * CY + y, 1), :]
                B[x, y] = b
            return 0

        lax.fori_loop(0, CX, body, 0)

    over_blocks(lambda x, y: source_copy(x, y).wait())
    add_nodes(incident[...], False)

    for side in range(6):
        k_copy(side).wait_recv()
    v, r, c = plan.v, plan.r, plan.c
    inside = [
        jnp.where(v == plan.n_vol - 1, 0.0, 1.0), jnp.where(v == 0, 0.0, 1.0),
        jnp.where(r == plan.n_row - 1, 0.0, 1.0), jnp.where(r == 0, 0.0, 1.0),
        jnp.where(c == plan.n_col - 1, 0.0, 1.0), jnp.where(c == 0, 0.0, 1.0),
    ]
    for x in range(CX):
        k = KC[x + 1]
        edge = [
            jnp.full((8, 128), x == CX - 1), jnp.full((8, 128), x == 0),
            subs == CY - 1, subs == 0, lanes == CZ - 1, lanes == 0,
        ]
        beyond = [
            KC[x + 2], KC[x],
            jnp.where(edge[2], jnp.broadcast_to(KYR[1, x : x + 1, :], (8, 128)), pltpu.roll(k, 7, 0)),
            jnp.where(edge[3], jnp.broadcast_to(KYR[0, x : x + 1, :], (8, 128)), pltpu.roll(k, 1, 0)),
            jnp.where(edge[4], pltpu.roll(KZR[1], 127 - x, 1), pltpu.roll(k, 127, 1)),
            jnp.where(edge[5], pltpu.roll(KZR[0], (128 - x) % 128, 1), pltpu.roll(k, 1, 1)),
        ]
        keep = []
        for side in range(6):
            if side >= 2 or (x == CX - 1 and side == 0) or (x == 0 and side == 1):
                keep.append(jnp.where(edge[side], inside[side], 1.0))
            else:
                keep.append(None)
        faces = []
        for side in range(6):
            other = beyond[side] if keep[side] is None else beyond[side] * keep[side]
            faces.append(0.5 * (k + other))
        diag = MASS_TERM + faces[0]
        for face in faces[1:]:
            diag = diag + face
        inverse = 1.0 / diag
        DI[x * CY : (x + 1) * CY, :] = inverse
        for side in range(6):
            face = faces[side] if keep[side] is None else faces[side] * keep[side]
            CO[side, x * CY : (x + 1) * CY, :] = face * inverse

    def pack(lane, value, down, up):
        here = lanes == lane
        down = jnp.where(here, pltpu.roll(value, lane, 1), down)
        up = jnp.where(here, pltpu.roll(value, lax.rem(lane + 1, 128), 1), up)
        return down, up

    def sweep(step):
        weight = weights[step]
        last = step == STEPS - 1
        if step > 0:
            for side in range(6):
                h_copy(step - 1, side).wait_recv()

            def spread(x, _):
                F[step - 1, x + 1, 0] = YR[step - 1, 0, x].astype(F32)
                F[step - 1, x + 1, CY + 1] = YR[step - 1, 1, x].astype(F32)
                return 0

            lax.fori_loop(0, CX, spread, 0)
            z_up, z_down = ZR[step - 1, 1], ZR[step - 1, 0]

        def body(x, carry):
            down, up = carry
            for y in range(CY):
                at = x * CY + y
                if step > 0:
                    co = [jnp.broadcast_to(CO[side, pl.ds(at, 1), :], (8, 128)) for side in range(6)]
                halves = []
                for h in range(2):
                    rows_h = pl.ds(8 * h, 8)
                    lane = x * 16 + (y * 2 + h)
                    if step == 0:
                        b = B[x, y, rows_h, :] * DI[pl.ds(at, 1), :]
                        B[x, y, rows_h, :] = b
                        new = weight * b
                    else:
                        value = F[step - 1, x + 1, y + 1, rows_h, :]
                        zp = jnp.where(
                            lanes == CZ - 1, pltpu.roll(z_up, 127 - lane, 1), pltpu.roll(value, 127, 1)
                        )
                        zm = jnp.where(
                            lanes == 0, pltpu.roll(z_down, lax.rem(128 - lane, 128), 1), pltpu.roll(value, 1, 1)
                        )
                        total = B[x, y, rows_h, :] + co[0] * F[step - 1, x + 2, y + 1, rows_h, :]
                        total = total + co[1] * F[step - 1, x, y + 1, rows_h, :]
                        total = total + co[2] * F[step - 1, x + 1, y + 2, rows_h, :]
                        total = total + co[3] * F[step - 1, x + 1, y, rows_h, :]
                        total = total + co[4] * zp
                        total = total + co[5] * zm
                        new = (1.0 - weight) * value + weight * total
                    F[step, x + 1, y + 1, rows_h, :] = new
                    if not last:
                        down, up = pack(lane, new, down, up)
                    halves.append(new)
                if not last and y in (0, CY - 1):
                    YS[step, 0 if y else 1, x] = jnp.concatenate(halves, axis=0).astype(BF16)
            return down, up

        zero = jnp.zeros((8, 128), F32)
        down, up = lax.fori_loop(0, CX, body, (zero, zero))
        if not last:
            ZS[step, 0] = up
            ZS[step, 1] = down

    def send_halos(step):
        for side in y_first:
            h_copy(step, side).start()

    g_steps = n_z * (ND // 16)

    def spread_positions():
        for delta in far_first:
            pz_copy(delta).wait_recv()
        for delta in plan.p_deltas:
            if delta != (0, 0):
                pp_copy(delta).wait_recv()

        def body(slot, _):
            wide = jnp.concatenate([POSZ[slot]] * 16, axis=0).T
            for axis in range(3):
                PJ[slot, axis] = jnp.broadcast_to(wide[:, axis : axis + 1], (ND, 128))
            return 0

        lax.fori_loop(0, n_z, body, 0)

    soft = SOFTENING * SOFTENING * inverse_scale * inverse_scale

    def build(first, past):
        def body(t, _):
            slot, group = lax.div(t, 8), lax.rem(t, 8)
            q, half = lax.div(slot, 2), lax.rem(slot, 2)
            mine = [PJ[slot, axis, pl.ds(group * 16, 16), :] for axis in range(3)]
            for n in range(n_p):
                dx, dy, dz = (
                    mine[axis] - jnp.broadcast_to(POSP[n, axis : axis + 1, :], (16, 128)) for axis in range(3)
                )
                squared = dx * dx + dy * dy + dz * dz
                tile = lax.rsqrt(squared + soft).astype(BF16)
                G[q, n // 2, pl.ds(half * ND + group * 16, 16), (n % 2) * ND : (n % 2 + 1) * ND] = tile
            return 0

        lax.fori_loop(first, past, body, 0)

    def read_traces(it, step):
        def body(x, acc):
            block = F[step, x + 1, pl.ds(1, CY)].reshape(CY * E, CZ).astype(BF16)
            at_nodes = jnp.dot(block, OH[...], preferred_element_type=F32)
            for y in range(CY):
                acc = jnp.where(rows16 == x * CY + y, at_nodes[y * E : (y + 1) * E], acc)
            return acc

        traces = lax.fori_loop(0, CX, body, jnp.zeros((E, ND), F32))
        own = plan.z_own
        TR[it, own // 2, :, (own % 2) * ND : (own % 2 + 1) * ND] = traces.astype(BF16)
        for delta in far_first:
            t_copy(it, delta).start()

    def product(it):
        for q in range(n_q):
            for slot in (2 * q, 2 * q + 1):
                if slot != plan.z_own:
                    delta = (n_z - plan.z_deltas[slot]) % n_z
                    t_copy(it, delta).wait_recv()
            left = TR[it, q]

            def tile(m, fresh=(q == 0), q=q, left=left):
                part = jnp.dot(left, G[q, m], preferred_element_type=F32)
                for side in range(2):
                    block = part[:, side * ND : (side + 1) * ND]
                    if fresh:
                        ACC[it, 2 * m + side] = block
                    else:
                        ACC[it, 2 * m + side] += block

            if q < n_q - 1:
                def body(m, _, tile=tile):
                    tile(m)
                    return 0

                lax.fori_loop(0, n_m, body, 0)
            else:
                for m in range(n_m):
                    tile(m)
                    for slot in (2 * m, 2 * m + 1):
                        if slot != plan.p_own:
                            r_copy(it, slot).start()
        total = ACC[it, plan.p_own]
        for slot in range(n_p):
            if slot != plan.p_own:
                r_copy(it, slot).wait_recv()
                total = total + RR[it, slot]
        return incident[...] + total

    sweep(0)
    send_halos(0)
    spread_positions()
    chunk = g_steps // (SWEEPS - 1)
    bounds = [0, chunk, 2 * chunk, g_steps]
    flux = None
    for it in range(ITERS):
        base = it * SWEEPS
        if it > 0:
            add_nodes(flux, True)
        for s in range(SWEEPS):
            step = base + s
            if step > 0:
                sweep(step)
                if s < SWEEPS - 1:
                    send_halos(step)
            if it == 0 and s < SWEEPS - 1:
                build(bounds[s], bounds[s + 1])
        read_traces(it, base + SWEEPS - 1)
        if it < ITERS - 1:
            send_halos(base + SWEEPS - 1)
        else:
            over_blocks(lambda x, y: field_copy(x, y).start())
        flux = product(it)
    flux_out[...] = flux

    over_blocks(lambda x, y: field_copy(x, y).wait())
    for side in range(6):
        k_copy(side).wait_send()
        for step in range(HALOS):
            h_copy(step, side).wait_send()
    for delta in far_first:
        pz_copy(delta).wait_send()
        for it in range(ITERS):
            t_copy(it, delta).wait_send()
    for slot, delta in enumerate(plan.p_deltas):
        if delta != (0, 0):
            pp_copy(delta).wait_send()
            for it in range(ITERS):
                r_copy(it, slot).wait_send()


def solution(mesh):
    plan = Plan(mesh)
    vmem = pl.BlockSpec(memory_space=pltpu.VMEM)
    smem = pl.BlockSpec(memory_space=pltpu.SMEM)
    hbm = pl.BlockSpec(memory_space=pl.ANY)
    dma = pltpu.SemaphoreType.DMA

    def per_device(source, labels, region_coeff, node_cell, node_pos, incident):
        return pl.pallas_call(
            functools.partial(kernel, plan),
            out_shape=(
                jax.ShapeDtypeStruct((E, CX, CY, CZ), F32),
                jax.ShapeDtypeStruct((E, ND), F32),
            ),
            in_specs=[hbm, vmem, smem, vmem, vmem, vmem],
            out_specs=(hbm, vmem),
            scratch_shapes=[
                pltpu.VMEM((STEPS, CX + 2, CY + 2, E, CZ), F32),
                pltpu.VMEM((CX, CY, E, CZ), F32),
                pltpu.VMEM((CX, CY, E, CZ), F32),
                pltpu.VMEM((CX + 2, CY, CZ), F32),
                pltpu.VMEM((2, CX, CZ), F32),
                pltpu.VMEM((2, CX, CZ), F32),
                pltpu.VMEM((2, 8, 128), F32),
                pltpu.VMEM((2, 8, 128), F32),
                pltpu.VMEM((6, CX * CY, CZ), F32),
                pltpu.VMEM((CX * CY, CZ), F32),
                pltpu.VMEM((HALOS, 2, CX, E, CZ), BF16),
                pltpu.VMEM((HALOS, 2, CX, E, CZ), BF16),
                pltpu.VMEM((HALOS, 2, 8, 128), F32),
                pltpu.VMEM((HALOS, 2, 8, 128), F32),
                pltpu.VMEM((CZ, ND), BF16),
                pltpu.VMEM((ITERS, plan.n_q, E, 2 * ND), BF16),
                pltpu.VMEM((ITERS, plan.n_p, E, ND), F32),
                pltpu.VMEM((ITERS, plan.n_p, E, ND), F32),
                pltpu.VMEM((plan.n_q, plan.n_m, 2 * ND, 2 * ND), BF16),
                pltpu.VMEM((plan.n_z, 8, ND), F32),
                pltpu.VMEM((plan.n_p, 8, ND), F32),
                pltpu.VMEM((plan.n_z, 3, ND, 128), F32),
                dma,
                dma,
                dma((6,)),
                dma((6,)),
                dma((HALOS, 6)),
                dma((HALOS, 6)),
                dma((plan.n_z,)),
                dma((plan.n_z,)),
                dma((plan.n_p,)),
                dma((plan.n_p,)),
                dma((ITERS, plan.n_z)),
                dma((ITERS, plan.n_z)),
                dma((ITERS, plan.n_p)),
                dma((ITERS, plan.n_p)),
            ],
            compiler_params=pltpu.CompilerParams(collective_id=0, has_side_effects=True),
            name="coupled",
        )(source, labels, region_coeff, node_cell.reshape(1, ND), node_pos, incident)

    placed = (
        P(None, "vol", "row", "col"),
        P("vol", "row", "col"),
        P(),
        P(("vol", "row", "col")),
        P(None, ("vol", "row", "col")),
        P(None, ("vol", "row", "col")),
    )
    return jax.shard_map(
        per_device,
        mesh=mesh,
        in_specs=placed,
        out_specs=(P(None, "vol", "row", "col"), P(None, ("vol", "row", "col"))),
        check_vma=False,
    )
```

```python
import functools
import math

import jax
import jax.numpy as jnp
from jax import lax
from jax.experimental import pallas as pl
from jax.experimental.pallas import tpu as pltpu
from jax.sharding import PartitionSpec as P

SWEEPS = 4
ITERS = 2

MASS_TERM = 0.05
SOFTENING = 0.05
KERNEL_GAIN = 2.0

MESH = pl.DeviceIdType.MESH
F32 = jnp.float32
BF16 = jnp.bfloat16

E, CX, CY, CZ, ND = 16, 8, 8, 128, 128
STEPS = SWEEPS * ITERS
HALOS = STEPS - 1
EDGE_GROUP, INNER_GROUP = 4, 2


def sweep_weights(count):
    return [
        1.0 / (1.05 - 0.95 * math.cos(math.pi * (2 * sweep + 1) / (2 * count)))
        for sweep in range(count)
    ]


class Plan:
    def __init__(self, mesh):
        self.n_vol, self.n_row, self.n_col = (mesh.shape[a] for a in ("vol", "row", "col"))
        self.z_hi = 4 if self.n_row == 16 else 2
        self.n_y = self.n_row // self.z_hi
        self.n_z = self.z_hi * self.n_col
        half = self.n_z // 2
        order = []
        for d in range(1, half):
            order += [d, self.n_z - d]
        order += [0, half]
        self.z_deltas = order
        self.z_own = order.index(0)
        self.n_q = self.n_z // 2
        ring = lambda d, n: min(d, n - d)
        plane = [(dv, dy) for dv in range(self.n_vol) for dy in range(self.n_y)]
        plane.sort(key=lambda p: -(ring(p[0], self.n_vol) / 2 + ring(p[1], self.n_y)))
        self.p_deltas = plane
        self.p_own = plane.index((0, 0))
        self.n_p = len(plane)
        self.n_m = self.n_p // 2
        self.nodes = ND * self.n_vol * self.n_row * self.n_col

    def here(self):
        v, r, c = (lax.axis_index(a) for a in ("vol", "row", "col"))
        self.v, self.r, self.c = v, r, c
        self.y = lax.div(r, self.z_hi)
        self.zh = lax.rem(r, self.z_hi)
        self.z = self.zh * self.n_col + c

    def z_peer(self, delta):
        zz = lax.rem(self.z + delta, self.n_z)
        return (self.v, self.y * self.z_hi + lax.div(zz, self.n_col), lax.rem(zz, self.n_col))

    def p_peer(self, delta):
        dv, dy = delta
        return (
            lax.rem(self.v + dv, self.n_vol),
            lax.rem(self.y + dy, self.n_y) * self.z_hi + self.zh,
            self.c,
        )

    def z_slot_of_me_at(self, delta):
        return self.z_deltas.index((self.n_z - delta) % self.n_z)

    def p_slot_of_me_at(self, delta):
        return self.p_deltas.index(((self.n_vol - delta[0]) % self.n_vol, (self.n_y - delta[1]) % self.n_y))

    def sides(self):
        up = lambda i, n: lax.rem(i + 1, n)
        down = lambda i, n: lax.rem(i + n - 1, n)
        v, r, c = self.v, self.r, self.c
        return (
            (up(v, self.n_vol), r, c),
            (down(v, self.n_vol), r, c),
            (v, up(r, self.n_row), c),
            (v, down(r, self.n_row), c),
            (v, r, up(c, self.n_col)),
            (v, r, down(c, self.n_col)),
        )


def kernel(
    plan, source, labels, coeff, cell, pos, incident, field_out, flux_out,
    F, S, B, KC, KYS, KYR, KZS, KZR, CO, DI, YS, YR, ZS, ZR, OH, TR, ACC, RR, G, POSZ, POSP, PJ,
    src_sem, k_ss, k_rs, h_ss, h_rs, pz_ss, pz_rs, pp_ss, pp_rs, t_ss, t_rs, r_ss, r_rs,
):
    plan.here()
    weights = sweep_weights(SWEEPS) * ITERS
    lanes = lax.broadcasted_iota(jnp.int32, (8, 128), 1)
    subs = lax.broadcasted_iota(jnp.int32, (8, 128), 0)
    sides = plan.sides()
    n_q, n_m, n_p, n_z = plan.n_q, plan.n_m, plan.n_p, plan.n_z

    def source_copy(x, y):
        return pltpu.make_async_copy(source.at[:, x, y, :], S.at[x, y], src_sem)

    def over_blocks(act):
        def body(x, _):
            for y in range(CY):
                act(x, y)
            return 0

        lax.fori_loop(0, CX, body, 0)

    over_blocks(lambda x, y: source_copy(x, y).start())

    barrier = pltpu.get_barrier_semaphore()
    peers = [plan.z_peer(d) for d in plan.z_deltas if d]
    peers += [plan.p_peer(d) for d in plan.p_deltas if d != (0, 0)]
    peers += [sides[2], sides[3]]
    for peer in peers:
        pl.semaphore_signal(barrier, inc=1, device_id=peer, device_id_type=MESH)

    kz_up = jnp.zeros((8, 128), F32)
    kz_down = jnp.zeros((8, 128), F32)
    for x in range(CX):
        label = labels[x]
        k = jnp.zeros((8, 128), F32)
        for region in range(8):
            k = jnp.where(label == region, coeff[region], k)
        KC[x + 1] = k
        KYS[0, x] = k[CY - 1]
        KYS[1, x] = k[0]
        kz_up = jnp.where(lanes == x, pltpu.roll(k, x + 1, 1), kz_up)
        kz_down = jnp.where(lanes == x, pltpu.roll(k, x, 1), kz_down)
    KZS[0] = kz_up
    KZS[1] = kz_down

    inverse_scale = math.sqrt(plan.nodes) / KERNEL_GAIN
    own_pos = pos[...] * inverse_scale
    POSZ[plan.z_own, 0:3, :] = own_pos
    POSP[plan.p_own, 0:3, :] = own_pos
    cells = jnp.broadcast_to(cell[...], (8, 128))
    rows = lax.div(cells, CZ)
    rows16 = jnp.concatenate([rows, rows], axis=0)
    z_of = lax.rem(cells, CZ)
    for block in range(CZ // 16):
        z_pair = jnp.concatenate([z_of - subs - 16 * block, z_of - subs - 16 * block - 8], axis=0)
        OH[16 * block : 16 * block + 16, :] = jnp.where(z_pair == 0, 1.0, 0.0).astype(BF16)

    pl.semaphore_wait(barrier, len(peers))

    def k_copy(side):
        src, dst = (
            (KC.at[CX], KC.at[0]),
            (KC.at[1], KC.at[CX + 1]),
            (KYS.at[0], KYR.at[0]),
            (KYS.at[1], KYR.at[1]),
            (KZS.at[0], KZR.at[0]),
            (KZS.at[1], KZR.at[1]),
        )[side]
        return pltpu.make_async_remote_copy(
            src_ref=src, dst_ref=dst, send_sem=k_ss.at[side], recv_sem=k_rs.at[side],
            device_id=sides[side], device_id_type=MESH,
        )

    def h_copy(step, side):
        inner = pl.ds(1, CY)
        src, dst = (
            (F.at[step, CX, inner], F.at[step, 0, inner]),
            (F.at[step, 1, inner], F.at[step, CX + 1, inner]),
            (YS.at[step, 0], YR.at[step, 0]),
            (YS.at[step, 1], YR.at[step, 1]),
            (ZS.at[step, 0], ZR.at[step, 0]),
            (ZS.at[step, 1], ZR.at[step, 1]),
        )[side]
        return pltpu.make_async_remote_copy(
            src_ref=src, dst_ref=dst, send_sem=h_ss.at[step, side], recv_sem=h_rs.at[step, side],
            device_id=sides[side], device_id_type=MESH,
        )

    def pz_copy(delta):
        slot = plan.z_slot_of_me_at(delta)
        return pltpu.make_async_remote_copy(
            src_ref=POSZ.at[plan.z_own, pl.ds(0, 3)], dst_ref=POSZ.at[slot, pl.ds(0, 3)], send_sem=pz_ss.at[slot], recv_sem=pz_rs.at[slot],
            device_id=plan.z_peer(delta), device_id_type=MESH,
        )

    def pp_copy(delta):
        slot = plan.p_slot_of_me_at(delta)
        return pltpu.make_async_remote_copy(
            src_ref=POSP.at[plan.p_own, pl.ds(0, 3)], dst_ref=POSP.at[slot, pl.ds(0, 3)], send_sem=pp_ss.at[slot], recv_sem=pp_rs.at[slot],
            device_id=plan.p_peer(delta), device_id_type=MESH,
        )

    def t_slot(it, slot):
        return TR.at[it, slot // 2, :, pl.ds((slot % 2) * ND, ND)]

    def t_copy(it, delta):
        slot = plan.z_slot_of_me_at(delta)
        return pltpu.make_async_remote_copy(
            src_ref=t_slot(it, plan.z_own), dst_ref=t_slot(it, slot), send_sem=t_ss.at[it, slot],
            recv_sem=t_rs.at[it, slot], device_id=plan.z_peer(delta), device_id_type=MESH,
        )

    def r_copy(it, slot):
        return pltpu.make_async_remote_copy(
            src_ref=ACC.at[it, slot], dst_ref=RR.at[it, slot], send_sem=r_ss.at[it, slot],
            recv_sem=r_rs.at[it, slot], device_id=plan.p_peer(plan.p_deltas[slot]), device_id_type=MESH,
        )

    flights = {}

    def launch(copy, *key):
        flight = copy(*key)
        flight.start()
        flights[(copy, *key)] = [flight, False]

    def arrive(copy, *key):
        entry = flights[(copy, *key)]
        entry[0].wait_recv()
        entry[1] = True

    y_first = (2, 3, 0, 1, 4, 5)
    far_first = sorted((d for d in plan.z_deltas if d), key=lambda d: -min(d, n_z - d))
    for side in y_first:
        launch(k_copy, side)
    for delta in far_first:
        launch(pz_copy, delta)
    for delta in plan.p_deltas:
        if delta != (0, 0):
            launch(pp_copy, delta)

    def add_nodes(flux, scaled):
        hi = flux.astype(BF16).astype(F32)
        low = flux - hi

        def body(x, _):
            total = jnp.zeros((CY * E, CZ), F32)
            for part in (hi, low):
                picked = [jnp.where(rows16 == x * CY + y, part, 0.0) for y in range(CY)]
                left = jnp.concatenate(picked, axis=0).astype(BF16)
                total = total + lax.dot_general(
                    left, OH[...], (((1,), (1,)), ((), ())), preferred_element_type=F32
                )
            for y in range(CY):
                b = S[x, y] + total[y * E : (y + 1) * E]
                if scaled:
                    b = b * DI[pl.ds(x * CY + y, 1), :]
                B[x, y] = b
            return 0

        lax.fori_loop(0, CX, body, 0, unroll=True)

    soft = SOFTENING * SOFTENING * inverse_scale * inverse_scale

    def build(first, past):
        for slot in range(first // 8, (past + 7) // 8):
            if slot * 8 >= first:
                if slot != plan.z_own:
                    arrive(pz_copy, (n_z - plan.z_deltas[slot]) % n_z)
                columns = POSZ[slot]
                wide = jnp.concatenate([columns] * 16, axis=0).T
                for axis in range(3):
                    PJ[slot, axis] = jnp.broadcast_to(wide[:, axis : axis + 1], (ND, 128))

        def body(t, _):
            slot, group = lax.div(t, 8), lax.rem(t, 8)
            q, half = lax.div(slot, 2), lax.rem(slot, 2)
            mine = [PJ[slot, axis, pl.ds(group * 16, 16), :] for axis in range(3)]
            for n in range(n_p):
                dx, dy, dz = (
                    mine[axis] - jnp.broadcast_to(POSP[n, axis : axis + 1, :], (16, 128)) for axis in range(3)
                )
                squared = dx * dx + dy * dy + dz * dz
                tile = lax.rsqrt(squared + soft).astype(BF16)
                G[q, n // 2, pl.ds(half * ND + group * 16, 16), (n % 2) * ND : (n % 2 + 1) * ND] = tile
            return 0

        lax.fori_loop(first, past, body, 0)

    over_blocks(lambda x, y: source_copy(x, y).wait())
    add_nodes(incident[...], False)
    for delta in plan.p_deltas:
        if delta != (0, 0):
            arrive(pp_copy, delta)
    g_steps = n_z * (ND // 16)
    bounds = [g_steps * part // 16 for part in (2, 5, 9, 12)]
    build(0, bounds[0])

    for side in range(6):
        arrive(k_copy, side)
    v, r, c = plan.v, plan.r, plan.c
    inside = [
        jnp.where(v == plan.n_vol - 1, 0.0, 1.0), jnp.where(v == 0, 0.0, 1.0),
        jnp.where(r == plan.n_row - 1, 0.0, 1.0), jnp.where(r == 0, 0.0, 1.0),
        jnp.where(c == plan.n_col - 1, 0.0, 1.0), jnp.where(c == 0, 0.0, 1.0),
    ]
    for x in range(CX):
        k = KC[x + 1]
        edge = [
            jnp.full((8, 128), x == CX - 1), jnp.full((8, 128), x == 0),
            subs == CY - 1, subs == 0, lanes == CZ - 1, lanes == 0,
        ]
        beyond = [
            KC[x + 2], KC[x],
            jnp.where(edge[2], jnp.broadcast_to(KYR[1, x : x + 1, :], (8, 128)), pltpu.roll(k, 7, 0)),
            jnp.where(edge[3], jnp.broadcast_to(KYR[0, x : x + 1, :], (8, 128)), pltpu.roll(k, 1, 0)),
            jnp.where(edge[4], pltpu.roll(KZR[1], 127 - x, 1), pltpu.roll(k, 127, 1)),
            jnp.where(edge[5], pltpu.roll(KZR[0], (128 - x) % 128, 1), pltpu.roll(k, 1, 1)),
        ]
        keep = []
        for side in range(6):
            if side >= 2 or (x == CX - 1 and side == 0) or (x == 0 and side == 1):
                keep.append(jnp.where(edge[side], inside[side], 1.0))
            else:
                keep.append(None)
        faces = []
        for side in range(6):
            other = beyond[side] if keep[side] is None else beyond[side] * keep[side]
            faces.append(0.5 * (k + other))
        diag = MASS_TERM + faces[0]
        for face in faces[1:]:
            diag = diag + face
        inverse = 1.0 / diag
        DI[x * CY : (x + 1) * CY, :] = inverse
        for side in range(6):
            face = faces[side] if keep[side] is None else faces[side] * keep[side]
            CO[side, x * CY : (x + 1) * CY, :] = face * inverse

    def turn(value, lanes_up):
        return pltpu.roll(value, lanes_up % 128, 1) if lanes_up % 128 else value

    def sweep(step, hold=False):
        weight = weights[step]
        last = step == STEPS - 1
        zero = jnp.zeros((8, 128), F32)
        if step > 0:
            for side in range(6):
                arrive(h_copy, step - 1, side)

            def spread(x, _):
                F[step - 1, x + 1, 0] = YR[step - 1, 0, x].astype(F32)
                F[step - 1, x + 1, CY + 1] = YR[step - 1, 1, x].astype(F32)
                return 0

            lax.fori_loop(0, CX, spread, 0)

        def body(i, carry, ys, group):
            down, up, z_up, z_down = carry
            for u in range(group):
                x = i * group + u
                for y in ys:
                    at = x * CY + y
                    if step > 0:
                        co = [jnp.broadcast_to(CO[side, pl.ds(at, 1), :], (8, 128)) for side in range(6)]
                    halves = []
                    for h in range(2):
                        rows_h = pl.ds(8 * h, 8)
                        local = u * 16 + y * 2 + h
                        if step == 0:
                            b = B[x, y, rows_h, :] * DI[pl.ds(at, 1), :]
                            B[x, y, rows_h, :] = b
                            new = weight * b
                        else:
                            value = F[step - 1, x + 1, y + 1, rows_h, :]
                            zp = jnp.where(lanes == CZ - 1, turn(z_up, 127 - local), turn(value, 127))
                            zm = jnp.where(lanes == 0, turn(z_down, 129 - local), turn(value, 1))
                            total = B[x, y, rows_h, :] + co[0] * F[step - 1, x + 2, y + 1, rows_h, :]
                            total = total + co[1] * F[step - 1, x, y + 1, rows_h, :]
                            total = total + co[2] * F[step - 1, x + 1, y + 2, rows_h, :]
                            total = total + co[3] * F[step - 1, x + 1, y, rows_h, :]
                            total = total + co[4] * zp
                            total = total + co[5] * zm
                            new = (1.0 - weight) * value + weight * total
                        if last:
                            field_out[x, y, rows_h, :] = new
                        else:
                            F[step, x + 1, y + 1, rows_h, :] = new
                            lane = i * (16 * group) + local
                            turned = pltpu.roll(new, lane, 1)
                            down = jnp.where(lanes == lane, turned, down)
                            up = jnp.where(lanes == (lane + 127) % 128, turned, up)
                        halves.append(new)
                    if not last and y in (0, CY - 1):
                        YS[step, 0 if y else 1, x] = jnp.concatenate(halves, axis=0).astype(BF16)
            if step > 0:
                z_up, z_down = turn(z_up, -16 * group), turn(z_down, -16 * group)
            return down, up, z_up, z_down

        def every(ys, group, carry):
            return lax.fori_loop(0, CX // group, functools.partial(body, ys=ys, group=group), carry)

        beyond_z = (ZR[step - 1, 1], ZR[step - 1, 0]) if step > 0 else (zero, zero)
        carry = every((0, CY - 1), EDGE_GROUP, (zero, zero) + beyond_z)
        if not last and not hold:
            for side in (2, 3):
                launch(h_copy, step, side)
        down, up, _, _ = every(range(1, CY - 1), INNER_GROUP, carry)
        if not last:
            ZS[step, 0] = up
            ZS[step, 1] = down
            if not hold:
                for side in (0, 1, 4, 5):
                    launch(h_copy, step, side)

    def send_halos(step):
        for side in y_first:
            launch(h_copy, step, side)

    def read_traces(it, step):
        def body(x, acc):
            block = field_out[x] if step == STEPS - 1 else F[step, x + 1, pl.ds(1, CY)]
            block = block.reshape(CY * E, CZ).astype(BF16)
            at_nodes = jnp.dot(block, OH[...], preferred_element_type=F32)
            for y in range(CY):
                acc = jnp.where(rows16 == x * CY + y, at_nodes[y * E : (y + 1) * E], acc)
            return acc

        traces = lax.fori_loop(0, CX, body, jnp.zeros((E, ND), F32), unroll=True)
        own = plan.z_own
        TR[it, own // 2, :, (own % 2) * ND : (own % 2 + 1) * ND] = traces.astype(BF16)
        for delta in far_first:
            launch(t_copy, it, delta)

    def product(it):
        for q in range(n_q):
            for slot in (2 * q, 2 * q + 1):
                if slot != plan.z_own:
                    delta = (n_z - plan.z_deltas[slot]) % n_z
                    arrive(t_copy, it, delta)
            left = TR[it, q]

            for m in range(n_m):
                part = jnp.dot(left, G[q, m], preferred_element_type=F32)
                for side in range(2):
                    block = part[:, side * ND : (side + 1) * ND]
                    if q == 0:
                        ACC[it, 2 * m + side] = block
                    else:
                        ACC[it, 2 * m + side] += block
                    if q == n_q - 1 and 2 * m + side != plan.p_own:
                        launch(r_copy, it, 2 * m + side)
        total = ACC[it, plan.p_own]
        for slot in range(n_p):
            if slot != plan.p_own:
                arrive(r_copy, it, slot)
                total = total + RR[it, slot]
        return incident[...] + total

    sweep(0)
    flux = None
    for it in range(ITERS):
        base = it * SWEEPS
        if it > 0:
            add_nodes(flux, True)
        for s in range(SWEEPS):
            step = base + s
            if step > 0:
                sweep(step, hold=s == SWEEPS - 1)
            if it == 0 and s < SWEEPS - 1:
                build(bounds[s], bounds[s + 1])
        read_traces(it, base + SWEEPS - 1)
        if it < ITERS - 1:
            send_halos(base + SWEEPS - 1)
            build(bounds[-1], g_steps)
        flux = product(it)
    flux_out[...] = flux

    for flight, arrived in flights.values():
        if not arrived:
            flight.wait_recv()
        flight.wait_send()


def write_out(field, flux, field_out, flux_out, field_sem, flux_sem):
    flux_copy = pltpu.make_async_copy(flux, flux_out, flux_sem)
    flux_copy.start()
    copies = [
        pltpu.make_async_copy(field.at[x, y], field_out.at[:, x, y, :], field_sem)
        for x in range(CX)
        for y in range(CY)
    ]
    for copy in copies:
        copy.start()
    for copy in copies:
        copy.wait()
    flux_copy.wait()


def solution(mesh):
    plan = Plan(mesh)
    vmem = pl.BlockSpec(memory_space=pltpu.VMEM)
    smem = pl.BlockSpec(memory_space=pltpu.SMEM)
    hbm = pl.BlockSpec(memory_space=pl.ANY)
    dma = pltpu.SemaphoreType.DMA

    def per_device(source, labels, region_coeff, node_cell, node_pos, incident):
        field, flux = pl.pallas_call(
            functools.partial(kernel, plan),
            out_shape=(
                jax.ShapeDtypeStruct((CX, CY, E, CZ), F32),
                jax.ShapeDtypeStruct((E, ND), F32),
            ),
            in_specs=[hbm, vmem, smem, vmem, vmem, vmem],
            out_specs=(vmem, vmem),
            scratch_shapes=[
                pltpu.VMEM((HALOS, CX + 2, CY + 2, E, CZ), F32),
                pltpu.VMEM((CX, CY, E, CZ), F32),
                pltpu.VMEM((CX, CY, E, CZ), F32),
                pltpu.VMEM((CX + 2, CY, CZ), F32),
                pltpu.VMEM((2, CX, CZ), F32),
                pltpu.VMEM((2, CX, CZ), F32),
                pltpu.VMEM((2, 8, 128), F32),
                pltpu.VMEM((2, 8, 128), F32),
                pltpu.VMEM((6, CX * CY, CZ), F32),
                pltpu.VMEM((CX * CY, CZ), F32),
                pltpu.VMEM((HALOS, 2, CX, E, CZ), BF16),
                pltpu.VMEM((HALOS, 2, CX, E, CZ), BF16),
                pltpu.VMEM((HALOS, 2, 8, 128), F32),
                pltpu.VMEM((HALOS, 2, 8, 128), F32),
                pltpu.VMEM((CZ, ND), BF16),
                pltpu.VMEM((ITERS, plan.n_q, E, 2 * ND), BF16),
                pltpu.VMEM((ITERS, plan.n_p, E, ND), F32),
                pltpu.VMEM((ITERS, plan.n_p, E, ND), F32),
                pltpu.VMEM((plan.n_q, plan.n_m, 2 * ND, 2 * ND), BF16),
                pltpu.VMEM((plan.n_z, 8, ND), F32),
                pltpu.VMEM((plan.n_p, 8, ND), F32),
                pltpu.VMEM((plan.n_z, 3, ND, 128), F32),
                dma,
                dma((6,)),
                dma((6,)),
                dma((HALOS, 6)),
                dma((HALOS, 6)),
                dma((plan.n_z,)),
                dma((plan.n_z,)),
                dma((plan.n_p,)),
                dma((plan.n_p,)),
                dma((ITERS, plan.n_z)),
                dma((ITERS, plan.n_z)),
                dma((ITERS, plan.n_p)),
                dma((ITERS, plan.n_p)),
            ],
            compiler_params=pltpu.CompilerParams(collective_id=0, has_side_effects=True),
            name="coupled",
        )(source, labels, region_coeff, node_cell.reshape(1, ND), node_pos, incident)
        return pl.pallas_call(
            write_out,
            out_shape=(
                jax.ShapeDtypeStruct((E, CX, CY, CZ), F32),
                jax.ShapeDtypeStruct((E, ND), F32),
            ),
            in_specs=[vmem, vmem],
            out_specs=(hbm, hbm),
            scratch_shapes=[dma, dma],
            name="write_out",
        )(field, flux)

    placed = (
        P(None, "vol", "row", "col"),
        P("vol", "row", "col"),
        P(),
        P(("vol", "row", "col")),
        P(None, ("vol", "row", "col")),
        P(None, ("vol", "row", "col")),
    )
    return jax.shard_map(
        per_device,
        mesh=mesh,
        in_specs=placed,
        out_specs=(P(None, "vol", "row", "col"), P(None, ("vol", "row", "col"))),
        check_vma=False,
    )
```

```python
import functools
import math

import jax
import jax.numpy as jnp
from jax import lax
from jax.experimental import pallas as pl
from jax.experimental.pallas import tpu as pltpu
from jax.sharding import PartitionSpec as P

SWEEPS = 4
ITERS = 2

MASS_TERM = 0.05
SOFTENING = 0.05
KERNEL_GAIN = 2.0

MESH = pl.DeviceIdType.MESH
F32 = jnp.float32
BF16 = jnp.bfloat16

E, CX, CY, CZ, ND = 16, 8, 8, 128, 128
STEPS = SWEEPS * ITERS
HALOS = STEPS - 1
EDGE_GROUP, INNER_GROUP = 4, 2


def sweep_weights(count):
    return [
        1.0 / (1.05 - 0.95 * math.cos(math.pi * (2 * sweep + 1) / (2 * count)))
        for sweep in range(count)
    ]


class Plan:
    def __init__(self, mesh):
        self.n_vol, self.n_row, self.n_col = (mesh.shape[a] for a in ("vol", "row", "col"))
        self.z_hi = 4 if self.n_row == 16 else 2
        self.n_y = self.n_row // self.z_hi
        self.n_z = self.z_hi * self.n_col
        half = self.n_z // 2
        order = []
        for d in range(1, half):
            order += [d, self.n_z - d]
        order += [0, half]
        self.z_deltas = order
        self.z_own = order.index(0)
        self.n_q = self.n_z // 2
        ring = lambda d, n: min(d, n - d)
        plane = [(dv, dy) for dv in range(self.n_vol) for dy in range(self.n_y)]
        plane.sort(key=lambda p: -(ring(p[0], self.n_vol) / 2 + ring(p[1], self.n_y)))
        self.p_deltas = plane
        self.p_own = plane.index((0, 0))
        self.n_p = len(plane)
        self.n_m = self.n_p // 2
        self.nodes = ND * self.n_vol * self.n_row * self.n_col

    def here(self):
        v, r, c = (lax.axis_index(a) for a in ("vol", "row", "col"))
        self.v, self.r, self.c = v, r, c
        self.y = lax.div(r, self.z_hi)
        self.zh = lax.rem(r, self.z_hi)
        self.z = self.zh * self.n_col + c

    def z_peer(self, delta):
        zz = lax.rem(self.z + delta, self.n_z)
        return (self.v, self.y * self.z_hi + lax.div(zz, self.n_col), lax.rem(zz, self.n_col))

    def p_peer(self, delta):
        dv, dy = delta
        return (
            lax.rem(self.v + dv, self.n_vol),
            lax.rem(self.y + dy, self.n_y) * self.z_hi + self.zh,
            self.c,
        )

    def z_slot_of_me_at(self, delta):
        return self.z_deltas.index((self.n_z - delta) % self.n_z)

    def p_slot_of_me_at(self, delta):
        return self.p_deltas.index(((self.n_vol - delta[0]) % self.n_vol, (self.n_y - delta[1]) % self.n_y))

    def sides(self):
        up = lambda i, n: lax.rem(i + 1, n)
        down = lambda i, n: lax.rem(i + n - 1, n)
        v, r, c = self.v, self.r, self.c
        return (
            (up(v, self.n_vol), r, c),
            (down(v, self.n_vol), r, c),
            (v, up(r, self.n_row), c),
            (v, down(r, self.n_row), c),
            (v, r, up(c, self.n_col)),
            (v, r, down(c, self.n_col)),
        )


def kernel(
    plan, source, labels, coeff, cell, pos, incident, field_out, flux_out,
    F, S, B, KC, KYS, KYR, KZS, KZR, CO, DI, YS, YR, ZS, ZR, OH, TR, ACC, RR, G, POSZ, POSP, PJ,
    src_sem, k_ss, k_rs, h_ss, h_rs, pz_ss, pz_rs, pp_ss, pp_rs, t_ss, t_rs, r_ss, r_rs,
):
    plan.here()
    weights = sweep_weights(SWEEPS) * ITERS
    lanes = lax.broadcasted_iota(jnp.int32, (8, 128), 1)
    subs = lax.broadcasted_iota(jnp.int32, (8, 128), 0)
    sides = plan.sides()
    n_q, n_m, n_p, n_z = plan.n_q, plan.n_m, plan.n_p, plan.n_z

    def source_copy(x, y):
        return pltpu.make_async_copy(source.at[:, x, y, :], S.at[x, y], src_sem)

    def over_blocks(act):
        def body(x, _):
            for y in range(CY):
                act(x, y)
            return 0

        lax.fori_loop(0, CX, body, 0)

    over_blocks(lambda x, y: source_copy(x, y).start())

    barrier = pltpu.get_barrier_semaphore()
    peers = [plan.z_peer(d) for d in plan.z_deltas if d]
    peers += [plan.p_peer(d) for d in plan.p_deltas if d != (0, 0)]
    peers += [sides[2], sides[3]]
    for peer in peers:
        pl.semaphore_signal(barrier, inc=1, device_id=peer, device_id_type=MESH)

    kz_up = jnp.zeros((8, 128), F32)
    kz_down = jnp.zeros((8, 128), F32)
    for x in range(CX):
        label = labels[x]
        k = jnp.zeros((8, 128), F32)
        for region in range(8):
            k = jnp.where(label == region, coeff[region], k)
        KC[x + 1] = k
        KYS[0, x] = k[CY - 1]
        KYS[1, x] = k[0]
        kz_up = jnp.where(lanes == x, pltpu.roll(k, x + 1, 1), kz_up)
        kz_down = jnp.where(lanes == x, pltpu.roll(k, x, 1), kz_down)
    KZS[0] = kz_up
    KZS[1] = kz_down

    inverse_scale = math.sqrt(plan.nodes) / KERNEL_GAIN
    own_pos = pos[...] * inverse_scale
    POSZ[plan.z_own, 0:3, :] = own_pos
    POSP[plan.p_own, 0:3, :] = own_pos
    cells = jnp.broadcast_to(cell[...], (8, 128))
    rows = lax.div(cells, CZ)
    rows16 = jnp.concatenate([rows, rows], axis=0)
    z_of = lax.rem(cells, CZ)
    for block in range(CZ // 16):
        z_pair = jnp.concatenate([z_of - subs - 16 * block, z_of - subs - 16 * block - 8], axis=0)
        OH[16 * block : 16 * block + 16, :] = jnp.where(z_pair == 0, 1.0, 0.0).astype(BF16)

    pl.semaphore_wait(barrier, len(peers))

    def k_copy(side):
        src, dst = (
            (KC.at[CX], KC.at[0]),
            (KC.at[1], KC.at[CX + 1]),
            (KYS.at[0], KYR.at[0]),
            (KYS.at[1], KYR.at[1]),
            (KZS.at[0], KZR.at[0]),
            (KZS.at[1], KZR.at[1]),
        )[side]
        return pltpu.make_async_remote_copy(
            src_ref=src, dst_ref=dst, send_sem=k_ss.at[side], recv_sem=k_rs.at[side],
            device_id=sides[side], device_id_type=MESH,
        )

    def h_copy(step, side):
        inner = pl.ds(1, CY)
        src, dst = (
            (F.at[step, CX, inner], F.at[step, 0, inner]),
            (F.at[step, 1, inner], F.at[step, CX + 1, inner]),
            (YS.at[step, 0], YR.at[step, 0]),
            (YS.at[step, 1], YR.at[step, 1]),
            (ZS.at[step, 0], ZR.at[step, 0]),
            (ZS.at[step, 1], ZR.at[step, 1]),
        )[side]
        return pltpu.make_async_remote_copy(
            src_ref=src, dst_ref=dst, send_sem=h_ss.at[step, side], recv_sem=h_rs.at[step, side],
            device_id=sides[side], device_id_type=MESH,
        )

    def pz_copy(delta):
        slot = plan.z_slot_of_me_at(delta)
        return pltpu.make_async_remote_copy(
            src_ref=POSZ.at[plan.z_own, pl.ds(0, 3)], dst_ref=POSZ.at[slot, pl.ds(0, 3)], send_sem=pz_ss.at[slot], recv_sem=pz_rs.at[slot],
            device_id=plan.z_peer(delta), device_id_type=MESH,
        )

    def pp_copy(delta):
        slot = plan.p_slot_of_me_at(delta)
        return pltpu.make_async_remote_copy(
            src_ref=POSP.at[plan.p_own, pl.ds(0, 3)], dst_ref=POSP.at[slot, pl.ds(0, 3)], send_sem=pp_ss.at[slot], recv_sem=pp_rs.at[slot],
            device_id=plan.p_peer(delta), device_id_type=MESH,
        )

    def t_slot(it, slot):
        return TR.at[it, slot // 2, :, pl.ds((slot % 2) * ND, ND)]

    def t_copy(it, delta):
        slot = plan.z_slot_of_me_at(delta)
        return pltpu.make_async_remote_copy(
            src_ref=t_slot(it, plan.z_own), dst_ref=t_slot(it, slot), send_sem=t_ss.at[it, slot],
            recv_sem=t_rs.at[it, slot], device_id=plan.z_peer(delta), device_id_type=MESH,
        )

    def r_copy(it, slot):
        return pltpu.make_async_remote_copy(
            src_ref=ACC.at[it, slot], dst_ref=RR.at[it, slot], send_sem=r_ss.at[it, slot],
            recv_sem=r_rs.at[it, slot], device_id=plan.p_peer(plan.p_deltas[slot]), device_id_type=MESH,
        )

    flights = {}

    def launch(copy, *key):
        flight = copy(*key)
        flight.start()
        flights[(copy, *key)] = [flight, False]

    def arrive(copy, *key):
        entry = flights[(copy, *key)]
        entry[0].wait_recv()
        entry[1] = True

    y_first = (2, 3, 0, 1, 4, 5)
    far_first = sorted((d for d in plan.z_deltas if d), key=lambda d: -min(d, n_z - d))
    for side in y_first:
        launch(k_copy, side)
    for delta in far_first:
        launch(pz_copy, delta)
    for delta in plan.p_deltas:
        if delta != (0, 0):
            launch(pp_copy, delta)

    def add_nodes(flux, scaled):
        hi = flux.astype(BF16).astype(F32)
        low = flux - hi

        def body(x, _):
            total = jnp.zeros((CY * E, CZ), F32)
            for part in (hi, low):
                picked = [jnp.where(rows16 == x * CY + y, part, 0.0) for y in range(CY)]
                left = jnp.concatenate(picked, axis=0).astype(BF16)
                total = total + lax.dot_general(
                    left, OH[...], (((1,), (1,)), ((), ())), preferred_element_type=F32
                )
            for y in range(CY):
                b = S[x, y] + total[y * E : (y + 1) * E]
                if scaled:
                    b = b * DI[pl.ds(x * CY + y, 1), :]
                B[x, y] = b
            return 0

        lax.fori_loop(0, CX, body, 0, unroll=True)

    soft = SOFTENING * SOFTENING * inverse_scale * inverse_scale

    def build(first, past):
        for slot in range(first // 8, (past + 7) // 8):
            if slot * 8 >= first:
                if slot != plan.z_own:
                    arrive(pz_copy, (n_z - plan.z_deltas[slot]) % n_z)
                columns = POSZ[slot]
                wide = jnp.concatenate([columns] * 16, axis=0).T
                for axis in range(3):
                    PJ[slot, axis] = jnp.broadcast_to(wide[:, axis : axis + 1], (ND, 128))

        def body(t, _):
            slot, group = lax.div(t, 8), lax.rem(t, 8)
            q, half = lax.div(slot, 2), lax.rem(slot, 2)
            mine = [PJ[slot, axis, pl.ds(group * 16, 16), :] for axis in range(3)]
            for n in range(n_p):
                dx, dy, dz = (
                    mine[axis] - jnp.broadcast_to(POSP[n, axis : axis + 1, :], (16, 128)) for axis in range(3)
                )
                squared = dx * dx + dy * dy + dz * dz
                tile = lax.rsqrt(squared + soft).astype(BF16)
                G[q, n // 2, pl.ds(half * ND + group * 16, 16), (n % 2) * ND : (n % 2 + 1) * ND] = tile
            return 0

        lax.fori_loop(first, past, body, 0)

    over_blocks(lambda x, y: source_copy(x, y).wait())
    add_nodes(incident[...], False)

    for side in range(6):
        arrive(k_copy, side)
    v, r, c = plan.v, plan.r, plan.c
    inside = [
        jnp.where(v == plan.n_vol - 1, 0.0, 1.0), jnp.where(v == 0, 0.0, 1.0),
        jnp.where(r == plan.n_row - 1, 0.0, 1.0), jnp.where(r == 0, 0.0, 1.0),
        jnp.where(c == plan.n_col - 1, 0.0, 1.0), jnp.where(c == 0, 0.0, 1.0),
    ]
    for x in range(CX):
        k = KC[x + 1]
        edge = [
            jnp.full((8, 128), x == CX - 1), jnp.full((8, 128), x == 0),
            subs == CY - 1, subs == 0, lanes == CZ - 1, lanes == 0,
        ]
        beyond = [
            KC[x + 2], KC[x],
            jnp.where(edge[2], jnp.broadcast_to(KYR[1, x : x + 1, :], (8, 128)), pltpu.roll(k, 7, 0)),
            jnp.where(edge[3], jnp.broadcast_to(KYR[0, x : x + 1, :], (8, 128)), pltpu.roll(k, 1, 0)),
            jnp.where(edge[4], pltpu.roll(KZR[1], 127 - x, 1), pltpu.roll(k, 127, 1)),
            jnp.where(edge[5], pltpu.roll(KZR[0], (128 - x) % 128, 1), pltpu.roll(k, 1, 1)),
        ]
        keep = []
        for side in range(6):
            if side >= 2 or (x == CX - 1 and side == 0) or (x == 0 and side == 1):
                keep.append(jnp.where(edge[side], inside[side], 1.0))
            else:
                keep.append(None)
        faces = []
        for side in range(6):
            other = beyond[side] if keep[side] is None else beyond[side] * keep[side]
            faces.append(0.5 * (k + other))
        diag = MASS_TERM + faces[0]
        for face in faces[1:]:
            diag = diag + face
        inverse = 1.0 / diag
        DI[x * CY : (x + 1) * CY, :] = inverse
        for side in range(6):
            face = faces[side] if keep[side] is None else faces[side] * keep[side]
            CO[side, x * CY : (x + 1) * CY, :] = face * inverse

    def turn(value, lanes_up):
        return pltpu.roll(value, lanes_up % 128, 1) if lanes_up % 128 else value

    def sweep(step, hold=False):
        weight = weights[step]
        last = step == STEPS - 1
        zero = jnp.zeros((8, 128), F32)
        if step > 0:
            for side in range(6):
                arrive(h_copy, step - 1, side)

            def spread(x, _):
                F[step - 1, x + 1, 0] = YR[step - 1, 0, x].astype(F32)
                F[step - 1, x + 1, CY + 1] = YR[step - 1, 1, x].astype(F32)
                return 0

            lax.fori_loop(0, CX, spread, 0)

        def body(i, carry, ys, group):
            down, up, z_up, z_down = carry
            for u in range(group):
                x = i * group + u
                for y in ys:
                    at = x * CY + y
                    if step > 0:
                        co = [jnp.broadcast_to(CO[side, pl.ds(at, 1), :], (8, 128)) for side in range(6)]
                    halves = []
                    for h in range(2):
                        rows_h = pl.ds(8 * h, 8)
                        local = u * 16 + y * 2 + h
                        if step == 0:
                            b = B[x, y, rows_h, :] * DI[pl.ds(at, 1), :]
                            B[x, y, rows_h, :] = b
                            new = weight * b
                        else:
                            value = F[step - 1, x + 1, y + 1, rows_h, :]
                            zp = jnp.where(lanes == CZ - 1, turn(z_up, 127 - local), turn(value, 127))
                            zm = jnp.where(lanes == 0, turn(z_down, 129 - local), turn(value, 1))
                            total = B[x, y, rows_h, :] + co[0] * F[step - 1, x + 2, y + 1, rows_h, :]
                            total = total + co[1] * F[step - 1, x, y + 1, rows_h, :]
                            total = total + co[2] * F[step - 1, x + 1, y + 2, rows_h, :]
                            total = total + co[3] * F[step - 1, x + 1, y, rows_h, :]
                            total = total + co[4] * zp
                            total = total + co[5] * zm
                            new = (1.0 - weight) * value + weight * total
                        if last:
                            field_out[x, y, rows_h, :] = new
                        else:
                            F[step, x + 1, y + 1, rows_h, :] = new
                            lane = i * (16 * group) + local
                            turned = pltpu.roll(new, lane, 1)
                            down = jnp.where(lanes == lane, turned, down)
                            up = jnp.where(lanes == (lane + 127) % 128, turned, up)
                        halves.append(new)
                    if not last and y in (0, CY - 1):
                        YS[step, 0 if y else 1, x] = jnp.concatenate(halves, axis=0).astype(BF16)
            if step > 0:
                z_up, z_down = turn(z_up, -16 * group), turn(z_down, -16 * group)
            return down, up, z_up, z_down

        def every(ys, group, carry):
            return lax.fori_loop(0, CX // group, functools.partial(body, ys=ys, group=group), carry)

        beyond_z = (ZR[step - 1, 1], ZR[step - 1, 0]) if step > 0 else (zero, zero)
        carry = every((0, CY - 1), EDGE_GROUP, (zero, zero) + beyond_z)
        if not last and not hold:
            for side in (2, 3):
                launch(h_copy, step, side)
        down, up, _, _ = every(range(1, CY - 1), INNER_GROUP, carry)
        if not last:
            ZS[step, 0] = up
            ZS[step, 1] = down
            if not hold:
                for side in (0, 1, 4, 5):
                    launch(h_copy, step, side)

    def send_halos(step):
        for side in y_first:
            launch(h_copy, step, side)

    def read_traces(it, step):
        def body(x, acc):
            block = field_out[x] if step == STEPS - 1 else F[step, x + 1, pl.ds(1, CY)]
            block = block.reshape(CY * E, CZ).astype(BF16)
            at_nodes = jnp.dot(block, OH[...], preferred_element_type=F32)
            for y in range(CY):
                acc = jnp.where(rows16 == x * CY + y, at_nodes[y * E : (y + 1) * E], acc)
            return acc

        traces = lax.fori_loop(0, CX, body, jnp.zeros((E, ND), F32), unroll=True)
        own = plan.z_own
        TR[it, own // 2, :, (own % 2) * ND : (own % 2 + 1) * ND] = traces.astype(BF16)
        for delta in far_first:
            launch(t_copy, it, delta)

    def product(it):
        for q in range(n_q):
            for slot in (2 * q, 2 * q + 1):
                if slot != plan.z_own:
                    delta = (n_z - plan.z_deltas[slot]) % n_z
                    arrive(t_copy, it, delta)
            left = TR[it, q]

            for m in range(n_m):
                part = jnp.dot(left, G[q, m], preferred_element_type=F32)
                for side in range(2):
                    block = part[:, side * ND : (side + 1) * ND]
                    if q == 0:
                        ACC[it, 2 * m + side] = block
                    else:
                        ACC[it, 2 * m + side] += block
                    if q == n_q - 1 and 2 * m + side != plan.p_own:
                        launch(r_copy, it, 2 * m + side)
        total = ACC[it, plan.p_own]
        for slot in range(n_p):
            if slot != plan.p_own:
                arrive(r_copy, it, slot)
                total = total + RR[it, slot]
        return incident[...] + total

    sweep(0)
    for delta in plan.p_deltas:
        if delta != (0, 0):
            arrive(pp_copy, delta)
    g_steps = n_z * (ND // 16)
    bounds = [g_steps * part // 16 for part in (0, 4, 8, 12)]
    flux = None
    for it in range(ITERS):
        base = it * SWEEPS
        if it > 0:
            add_nodes(flux, True)
        for s in range(SWEEPS):
            step = base + s
            if step > 0:
                sweep(step, hold=s == SWEEPS - 1)
            if it == 0 and s < SWEEPS - 1:
                build(bounds[s], bounds[s + 1])
        read_traces(it, base + SWEEPS - 1)
        if it < ITERS - 1:
            build(bounds[-1], g_steps)
            send_halos(base + SWEEPS - 1)
        flux = product(it)
    flux_out[...] = flux

    for flight, arrived in flights.values():
        if not arrived:
            flight.wait_recv()
        flight.wait_send()


def write_out(field, flux, field_out, flux_out, field_sem, flux_sem):
    flux_copy = pltpu.make_async_copy(flux, flux_out, flux_sem)
    flux_copy.start()
    copies = [
        pltpu.make_async_copy(field.at[x, y], field_out.at[:, x, y, :], field_sem)
        for x in range(CX)
        for y in range(CY)
    ]
    for copy in copies:
        copy.start()
    for copy in copies:
        copy.wait()
    flux_copy.wait()


def solution(mesh):
    plan = Plan(mesh)
    vmem = pl.BlockSpec(memory_space=pltpu.VMEM)
    smem = pl.BlockSpec(memory_space=pltpu.SMEM)
    hbm = pl.BlockSpec(memory_space=pl.ANY)
    dma = pltpu.SemaphoreType.DMA

    def per_device(source, labels, region_coeff, node_cell, node_pos, incident):
        field, flux = pl.pallas_call(
            functools.partial(kernel, plan),
            out_shape=(
                jax.ShapeDtypeStruct((CX, CY, E, CZ), F32),
                jax.ShapeDtypeStruct((E, ND), F32),
            ),
            in_specs=[hbm, vmem, smem, vmem, vmem, vmem],
            out_specs=(vmem, vmem),
            scratch_shapes=[
                pltpu.VMEM((HALOS, CX + 2, CY + 2, E, CZ), F32),
                pltpu.VMEM((CX, CY, E, CZ), F32),
                pltpu.VMEM((CX, CY, E, CZ), F32),
                pltpu.VMEM((CX + 2, CY, CZ), F32),
                pltpu.VMEM((2, CX, CZ), F32),
                pltpu.VMEM((2, CX, CZ), F32),
                pltpu.VMEM((2, 8, 128), F32),
                pltpu.VMEM((2, 8, 128), F32),
                pltpu.VMEM((6, CX * CY, CZ), F32),
                pltpu.VMEM((CX * CY, CZ), F32),
                pltpu.VMEM((HALOS, 2, CX, E, CZ), BF16),
                pltpu.VMEM((HALOS, 2, CX, E, CZ), BF16),
                pltpu.VMEM((HALOS, 2, 8, 128), F32),
                pltpu.VMEM((HALOS, 2, 8, 128), F32),
                pltpu.VMEM((CZ, ND), BF16),
                pltpu.VMEM((ITERS, plan.n_q, E, 2 * ND), BF16),
                pltpu.VMEM((ITERS, plan.n_p, E, ND), F32),
                pltpu.VMEM((ITERS, plan.n_p, E, ND), F32),
                pltpu.VMEM((plan.n_q, plan.n_m, 2 * ND, 2 * ND), BF16),
                pltpu.VMEM((plan.n_z, 8, ND), F32),
                pltpu.VMEM((plan.n_p, 8, ND), F32),
                pltpu.VMEM((plan.n_z, 3, ND, 128), F32),
                dma,
                dma((6,)),
                dma((6,)),
                dma((HALOS, 6)),
                dma((HALOS, 6)),
                dma((plan.n_z,)),
                dma((plan.n_z,)),
                dma((plan.n_p,)),
                dma((plan.n_p,)),
                dma((ITERS, plan.n_z)),
                dma((ITERS, plan.n_z)),
                dma((ITERS, plan.n_p)),
                dma((ITERS, plan.n_p)),
            ],
            compiler_params=pltpu.CompilerParams(collective_id=0, has_side_effects=True),
            name="coupled",
        )(source, labels, region_coeff, node_cell.reshape(1, ND), node_pos, incident)
        return pl.pallas_call(
            write_out,
            out_shape=(
                jax.ShapeDtypeStruct((E, CX, CY, CZ), F32),
                jax.ShapeDtypeStruct((E, ND), F32),
            ),
            in_specs=[vmem, vmem],
            out_specs=(hbm, hbm),
            scratch_shapes=[dma, dma],
            name="write_out",
        )(field, flux)

    placed = (
        P(None, "vol", "row", "col"),
        P("vol", "row", "col"),
        P(),
        P(("vol", "row", "col")),
        P(None, ("vol", "row", "col")),
        P(None, ("vol", "row", "col")),
    )
    return jax.shard_map(
        per_device,
        mesh=mesh,
        in_specs=placed,
        out_specs=(P(None, "vol", "row", "col"), P(None, ("vol", "row", "col"))),
        check_vma=False,
    )
```
